128 devices in a mesh: row: 16 (over y, z), col: 8 (over x, core).
Axes of the slice: x: 4, y: 4, z: 4, core: 2. Of those that a mesh axis runs over, the one named last changes fastest.
Arguments:
- voltages: float32 [4, 1, 2, 16384], P(None, None, None, ('row', 'col')), may hold values from -6 to 6
- antenna_gains: float32 [2, 16384], P(None, ('row', 'col')), may hold values from -5 to 5
- receiving_tile_index: int32 [4, 16384, 1], P(None, ('row', 'col')), may hold values from 0 to 127; in each aligned block of 128 rows (0 to 127, 128 to 255, ..., all dimensions but the last counted through in order) at most 3 rows name the same one
- cell_index: int32 [4, 16384], P(None, ('row', 'col')), may hold values from 0 to 131071
- beam_weights: float32 [4, 4096, 4096], P(None, ('row', 'col')), may hold values from 0.5 to 2000, as said below
Outputs:
- gain_gradient: float32 [2, 16384], P(None, ('row', 'col'))
The draws below stay inside these ranges and needn't reach their ends.
Inputs may be any that keep to these rules, and one draw needn't show every extreme that they name: `receiving_tile_index`: tile t covers grid rows from (t // 8) * 256 and columns from (t % 8) * 512; among the 128 antennas of one device in one channel at most 3 name the same tile. `cell_index`: the cell's row within the tile is cell // 512, its column cell % 512. `beam_weights`: positive weights.
All inputs are finite; a program needn't handle non-finite values.
Results may differ from the reference program's by a relative error of at most 0.0003.
Values sent between devices are 32-bit elements; how exact they have to be, the bound alone decides.
No kernel may reach another device: no remote copies, remote signals or barrier semaphores. Data moves between devices by JAX's collectives and lax.ppermute only.
A program may use at most 64 MiB of HBM per device.

```python
import math
import jax
import jax.numpy as jnp
import numpy as np

GRID_SIDE = 4096
CHANNEL_COUNT = 4
SAMPLES = 1
ANTENNA_DEVICE = 128
ANTENNA_TOTAL = 16384
TILE_CAPACITY = 3
TILE_R = 256
TILE_C = 512
N_ROW = 16
N_COL = 8
DEVICES = 128


def draw_beam_weights(key, part):
    key_col, key_cell = jax.random.split(key, 2)
    ramp_axis = jnp.arange(GRID_SIDE, dtype=jnp.float32) / GRID_SIDE
    ramp_top = jnp.log(10.0)
    col_part = jax.random.uniform(key_col, (CHANNEL_COUNT, 1, GRID_SIDE), jnp.float32, 0.0, 1.0) * jnp.log(10.0)
    rough_part = jax.random.uniform(key_cell, (CHANNEL_COUNT, GRID_SIDE, GRID_SIDE), jnp.float32, jnp.log(0.5), jnp.log(2.0))
    return jnp.exp(ramp_top * ramp_axis[None, :, None] + col_part + rough_part)


def place_ends(values, rng, smallest, largest):
    index_at = [jax.random.randint(jax.random.fold_in(rng, axis), (), 0, length) for axis, length in enumerate(values.shape)]
    widest = values.shape.index(max(values.shape))
    neighbour = index_at[:widest] + [(index_at[widest] + 1) % values.shape[widest]] + index_at[widest + 1:]
    return values.at[tuple(index_at)].set(smallest).at[tuple(neighbour)].set(largest)


def shard_levels(key, dims, cuts, least, high):
    level = 1.0
    for axis_at, blocks in cuts:
        draws = jax.random.uniform(jax.random.fold_in(jax.random.fold_in(key, 6), axis_at), (blocks,), jnp.float32, least / len(cuts), high / len(cuts))
        level = level * jnp.repeat(jnp.exp(draws), dims[axis_at] // blocks).reshape((-1,) + (1,) * (len(dims) - 1 - axis_at))
    return level


def routed_block(own_key, own, number, rows, number_of, top, reach, lean):
    ranking = jax.random.permutation(own_key, number_of)
    heavy_load, common = portions_of(number_of, rows * top, reach, lean, True), portions_of(number_of, rows * top, reach, lean, False)
    places = jnp.arange(number_of)

    def named(sizes, turn):
        used = int((sizes > 0).sum())
        fixed = max(1, used // 4)
        passed = fixed + (places - fixed + turn * (used - fixed)) % max(1, number_of - fixed)
        return jnp.zeros((number_of,), jnp.int32).at[ranking[jnp.where(places < fixed, places, passed)]].set(jnp.asarray(sizes, jnp.int32))

    sizes = jnp.where(number % 4 == 0, named(heavy_load, number // 4), named(common, number - number // 4 - 1))
    mixed = jax.random.permutation(jax.random.fold_in(own, 3), number_of)
    giver, receiver = mixed[0:number_of // 2 * 2:2], mixed[1:number_of // 2 * 2:2]
    margin = jnp.minimum(sizes[giver] - 1, reach - sizes[receiver]) // 2
    margin = jnp.where((giver == ranking[0]) | (receiver == ranking[0]) | (sizes[receiver] == 0), 0, jnp.maximum(margin, 0))
    passed = jax.random.randint(jax.random.fold_in(own, 4), (number_of // 2,), 0, 1 << 20) % (margin + 1)
    sizes = sizes.at[giver].add(-passed).at[receiver].add(passed)
    items = jnp.searchsorted(jnp.cumsum(sizes), jnp.arange(rows * top), side="right").astype(jnp.int32)
    listing = items.reshape(top, rows).T
    listing = listing[jax.random.permutation(jax.random.fold_in(own, 1), rows)]
    turn = jax.random.randint(jax.random.fold_in(own, 2), (rows, 1), 0, top)
    return jnp.take_along_axis(listing, (jnp.arange(top)[None, :] + turn) % top, axis=1)


def portions_of(number_of, total, limit, slope, full):
    loads = [(1 << 20) // math.isqrt(grade ** slope) + 1 for grade in range(1, number_of + 1)]
    largest = limit if full else min(limit, max(-(-total // number_of), total * loads[0] // sum(loads)))
    least = 1 if total - largest >= number_of - 1 else 0
    holding, spare = [largest] + [least] * (number_of - 1), total - largest - least * (number_of - 1)
    while spare > 0:
        free = [i for i in range(1, number_of) if holding[i] < largest] or [i for i in range(1, number_of) if holding[i] < limit]
        mass, remaining = sum([loads[i] for i in free]), spare
        for i in free:
            more = min(limit - holding[i], max(1, remaining * loads[i] // mass), spare)
            holding[i] = holding[i] + more
            spare = spare - more
    return np.array(holding)


def noise(stream_key, dims, deviation, bound, pieces=(), kind=jnp.bfloat16):
    values = jax.random.normal(stream_key, dims, jnp.float32) * deviation
    if len(pieces) > 0:
        values = shard_levels(stream_key, dims, pieces, -0.22, 0.18) * values
    return jnp.clip(values, min=-bound, max=bound).astype(kind)


def setup_inputs(seed: int = 0) -> dict:
    key_list = jax.random.split(jax.random.key(seed), 6)
    voltages = noise(key_list[0], (CHANNEL_COUNT, SAMPLES, 2, ANTENNA_TOTAL), 1.0, 6.0, ((3, 128),), jnp.float32)
    antenna_gains = noise(key_list[1], (2, ANTENNA_TOTAL), 1.0, 5.0, ((1, 128),), jnp.float32)
    receiving_tile_index_keys = jax.random.split(jax.random.fold_in(key_list[2], 1), CHANNEL_COUNT * ANTENNA_TOTAL // ANTENNA_DEVICE)
    receiving_tile_index_turns = jax.random.permutation(jax.random.fold_in(key_list[2], 3), CHANNEL_COUNT * ANTENNA_TOTAL // ANTENNA_DEVICE)
    receiving_tile_index = jax.vmap(lambda own, number: routed_block(jax.random.fold_in(key_list[2], 2), own, number, ANTENNA_DEVICE, DEVICES, 1, TILE_CAPACITY, 1))(receiving_tile_index_keys, receiving_tile_index_turns).reshape((CHANNEL_COUNT, ANTENNA_TOTAL, 1))
    cell_index = place_ends(jax.random.randint(key_list[3], (CHANNEL_COUNT, ANTENNA_TOTAL), 0, TILE_R * TILE_C), jax.random.fold_in(key_list[3], 1), 0, (TILE_R * TILE_C) - 1).astype(jnp.int32)
    beam_weights = draw_beam_weights(jax.random.fold_in(key_list[5], 71), 0)
    return {"voltages": voltages, "antenna_gains": antenna_gains, "receiving_tile_index": receiving_tile_index, "cell_index": cell_index, "beam_weights": beam_weights}


def reference(voltages, antenna_gains, receiving_tile_index, cell_index, beam_weights):
    tile_rows = GRID_SIDE // N_ROW
    tile_cols = GRID_SIDE // N_COL
    tile_ids = receiving_tile_index[:, :, 0]
    grid_row = (tile_ids // N_COL * tile_rows + cell_index // tile_cols).astype(jnp.int32)
    grid_col = (tile_ids % N_COL * tile_cols + cell_index % tile_cols).astype(jnp.int32)
    volt_re = voltages[:, :, 0]
    volt_im = voltages[:, :, 1]
    calib_re = antenna_gains[0] * volt_re - antenna_gains[1] * volt_im
    calib_im = antenna_gains[0] * volt_im + antenna_gains[1] * volt_re
    antennas = voltages.shape[3]
    loss_factor = float(GRID_SIDE) ** 3 * math.sqrt(antennas)
    grad_re = jnp.zeros(antennas, voltages.dtype)
    grad_im = jnp.zeros(antennas, voltages.dtype)
    for channel in range(CHANNEL_COUNT):
        spectra = []
        power_map = jnp.zeros((GRID_SIDE, GRID_SIDE), voltages.dtype)
        for sample in range(SAMPLES):
            aperture_re = jnp.zeros((GRID_SIDE, GRID_SIDE), voltages.dtype).at[grid_row[channel], grid_col[channel]].add(calib_re[channel, sample])
            aperture_im = jnp.zeros((GRID_SIDE, GRID_SIDE), voltages.dtype).at[grid_row[channel], grid_col[channel]].add(calib_im[channel, sample])
            spectrum = jnp.fft.fft2(aperture_re + 1j * aperture_im)
            spectra.append(spectrum)
            power_map = power_map + jnp.real(spectrum) ** 2 + jnp.imag(spectrum) ** 2
        beam_map = beam_weights[channel].T
        weighted = beam_map * power_map
        power_total = jnp.sum(weighted)
        power_square = jnp.sum(weighted * weighted)
        weight = 2.0 * loss_factor * beam_map * ((weighted - power_square / power_total) / (power_total * power_total))
        for sample in range(SAMPLES):
            adjoint = jnp.fft.ifft2(2.0 * weight * spectra[sample]) * float(GRID_SIDE * GRID_SIDE)
            picked = adjoint[grid_row[channel], grid_col[channel]]
            grad_re = grad_re + jnp.real(picked) * volt_re[channel, sample] + jnp.imag(picked) * volt_im[channel, sample]
            grad_im = grad_im + jnp.imag(picked) * volt_re[channel, sample] - jnp.real(picked) * volt_im[channel, sample]
    return jnp.stack((grad_re, grad_im))
```

```python
import math

import jax
import jax.numpy as jnp
import numpy as np
from jax import lax
from jax.experimental import pallas as pl
from jax.experimental.pallas import tpu as pltpu
from jax.sharding import PartitionSpec as P

GRID = 4096
AXES = ("row", "col")
CHANNELS = 4
LANES = 128
SOURCES = 128
BUCKETS = 16
CAP = 24
SLOTS = BUCKETS * CAP
WIDTH = 32
ROWS = 256

f32 = jnp.float32
bf16 = jnp.bfloat16
i32 = jnp.int32
NT = (((1,), (1,)), ((), ()))
NN = (((1,), (0,)), ((), ()))


def split_table(values):
    high = values.astype(np.float32).astype(jnp.bfloat16)
    low = (values - high.astype(np.float64)).astype(np.float32).astype(jnp.bfloat16)
    return high, low


def dft_tables():
    n = np.arange(ROWS)
    angle = 2.0 * np.pi * (np.outer(n, n) % ROWS) / ROWS
    cos, sin = np.cos(angle), np.sin(angle)
    matrix = np.block([[cos, -sin], [sin, cos]])
    high, low = split_table(matrix)
    turn = 2.0 * np.pi * np.outer(np.arange(BUCKETS), n) / GRID
    twiddle = np.stack([np.cos(turn), -np.sin(turn)]).astype(np.float32)
    return high, low, twiddle


def cmul(a, b):
    return (a[0] * b[0] - a[1] * b[1], a[0] * b[1] + a[1] * b[0])


def cadd(a, b):
    return (a[0] + b[0], a[1] + b[1])


def csub(a, b):
    return (a[0] - b[0], a[1] - b[1])


def cturn(a, sign):
    return (-a[1], a[0]) if sign > 0 else (a[1], -a[0])


def radix4(x, sign):
    s0, d0 = cadd(x[0], x[2]), csub(x[0], x[2])
    s1, d1 = cadd(x[1], x[3]), cturn(csub(x[1], x[3]), sign)
    return [cadd(s0, s1), cadd(d0, d1), csub(s0, s1), csub(d0, d1)]


def radix16(x, sign):
    inner = [radix4([x[4 * a + b] for a in range(4)], sign) for b in range(4)]
    out = [None] * 16
    for low in range(4):
        terms = []
        for b in range(4):
            value = inner[b][low]
            turns = (b * low) % 16
            if turns == 4:
                value = cturn(value, sign)
            elif turns:
                angle = sign * 2.0 * math.pi * turns / 16
                value = cmul(value, (math.cos(angle), math.sin(angle)))
            terms.append(value)
        result = radix4(terms, sign)
        for m in range(4):
            out[low + 4 * m] = result[m]
    return out


def unit_phase(steps):
    quarter = (steps + 512) >> 10
    x = (steps - (quarter << 10)).astype(f32) * (2.0 * math.pi / GRID)
    x2 = x * x
    sin = x * (1.0 + x2 * (-1.0 / 6 + x2 * (1.0 / 120 + x2 * (-1.0 / 5040 + x2 * (1.0 / 362880)))))
    cos = 1.0 + x2 * (
        -0.5 + x2 * (1.0 / 24 + x2 * (-1.0 / 720 + x2 * (1.0 / 40320 - x2 * (1.0 / 3628800))))
    )
    swap = (quarter & 1) == 1
    real = jnp.where(swap, sin, cos)
    imag = jnp.where(swap, cos, sin)
    real = jnp.where(((quarter + 1) & 2) == 2, -real, real)
    imag = jnp.where((quarter & 2) == 2, -imag, imag)
    return real, -imag


def lane_pick(values, index):
    return jnp.take_along_axis(values, index, axis=1)


def pack_kernel(volt_ref, gain_ref, tile_ref, cell_ref, message_ref, place_ref):
    lane = lax.broadcasted_iota(i32, (1, LANES), 1)
    down = lax.broadcasted_iota(i32, (LANES, LANES), 0).astype(f32)
    rows = [[], [], [], []]
    for c in range(CHANNELS):
        tile = tile_ref[c : c + 1, :]
        cell = cell_ref[c : c + 1, :]
        key = ((tile >> 3) * LANES + lane).astype(f32)
        key_across = jnp.broadcast_to(key, (LANES, LANES))
        key_down = key_across.T
        place = jnp.sum(jnp.where(key_down < key_across, 1.0, 0.0), axis=0, keepdims=True)
        place_ref[c : c + 1, :] = place.astype(i32)
        order = jnp.where(down == place, 1.0, 0.0)
        vr, vi = volt_ref[2 * c : 2 * c + 1, :], volt_ref[2 * c + 1 : 2 * c + 2, :]
        gr, gi = gain_ref[0:1, :], gain_ref[1:2, :]
        grid_row = ((tile >> 3) * ROWS + (cell >> 9)).astype(f32)
        grid_col = ((tile & 7) * 512 + (cell & 511)).astype(f32)
        features = jnp.concatenate(
            [gr * vr - gi * vi, gr * vi + gi * vr, grid_row, grid_col, jnp.zeros((4, LANES), f32)], 0
        )
        ordered = lax.dot_general(
            features, order, NT, precision=lax.Precision.HIGHEST, preferred_element_type=f32
        )
        for f in range(4):
            rows[f].append(ordered[f : f + 1, :])
    message = jnp.concatenate([row for group in rows for row in group], 0)

    def put(d, carry):
        message_ref[d] = message
        return carry

    lax.fori_loop(0, SOURCES, put, 0, unroll=8)


def slot_kernel(got_ref, vr_ref, vi_ref, row_ref, col_ref, back_ref, most_ref, buf, sems):
    outs = (vr_ref, vi_ref, row_ref, col_ref)

    def copies():
        return [
            pltpu.make_async_copy(got_ref.at[:, k, :], buf.at[k], sems.at[k]) for k in range(16)
        ]

    for copy in copies():
        copy.start()
    for copy in copies():
        copy.wait()
    lane = lax.broadcasted_iota(i32, (LANES, LANES), 1)
    most_ref[...] = jnp.zeros((8, LANES), i32)
    for c in range(CHANNELS):
        bucket = buf[8 + c].astype(i32) >> 8
        start = jnp.zeros((LANES, LANES), i32)
        for step in (64, 32, 16, 8, 4, 2, 1, 1):
            probe = start + step
            seen = lane_pick(bucket, probe - 1)
            start = jnp.where(seen < lane, probe, start)
        count = pltpu.roll(start, LANES - 1, axis=1) - start
        most_ref[c : c + 1, :] = jnp.max(count, axis=0, keepdims=True)
        back_ref[c] = bucket * CAP + lane - lane_pick(start, bucket)
        for t in range(3):
            slot = lane + t * LANES
            owner = (slot * 2731) >> 16
            rank = slot - owner * CAP
            source = jnp.minimum(lane_pick(start, owner) + rank, LANES - 1)
            valid = rank < lane_pick(count, owner)
            for f in range(4):
                picked = lane_pick(buf[4 * f + c], source)
                if f == 2:
                    picked = picked - owner.astype(f32) * ROWS
                picked = jnp.where(valid, picked, 0.0)
                outs[f][pl.ds(c * SLOTS + t * LANES, LANES), :] = picked.T


def fill_iota(iota_ref):
    iota_ref[...] = lax.broadcasted_iota(i32, (ROWS, LANES), 0).astype(f32).astype(bf16)


def one_hot(row_ref, iota_ref, at):
    want = jnp.broadcast_to(row_ref[pl.ds(at, 1), :], (16, LANES)).astype(bf16)
    one, zero = jnp.ones((16, LANES), bf16), jnp.zeros((16, LANES), bf16)
    return jnp.concatenate(
        [jnp.where(iota_ref[16 * i : 16 * i + 16, :] == want, one, zero) for i in range(ROWS // 16)], 0
    )


def two_terms(x):
    high = x.astype(bf16)
    return high, (x - high.astype(f32)).astype(bf16)


def phase_rows(tile, base, first, col_ref, br, bi, zr, zi, value=None):
    at = pl.multiple_of(base + 8 * tile, 8)
    col = col_ref[pl.ds(at, 8), :].astype(i32)
    b0 = unit_phase((col * first) & (GRID - 1))
    if value is not None:
        b0 = cmul((value[0][pl.ds(at, 8), :], value[1][pl.ds(at, 8), :]), b0)
    w1 = unit_phase(col)
    w2 = cmul(w1, w1)
    w4 = cmul(w2, w2)
    w8 = cmul(w4, w4)
    b = [b0, cmul(b0, w1)]
    b += [cmul(x, w2) for x in b]
    b += [cmul(x, w4) for x in b]
    for s in range(8):
        to = pl.multiple_of(64 * tile + 8 * s, 8)
        br[pl.ds(to, 8), :] = b[s][0]
        bi[pl.ds(to, 8), :] = b[s][1]
    to = pl.multiple_of(8 * tile, 8)
    zr[pl.ds(to, 8), :] = w8[0]
    zi[pl.ds(to, 8), :] = w8[1]


def load_phases(rank, br, bi, zr, zi):
    tile, inner = rank >> 3, rank & 7
    b = (br[pl.ds(64 * tile + inner, 8, stride=8), :], bi[pl.ds(64 * tile + inner, 8, stride=8), :])
    z = (
        jnp.broadcast_to(zr[pl.ds(rank, 1), :], (8, LANES)),
        jnp.broadcast_to(zi[pl.ds(rank, 1), :], (8, LANES)),
    )
    return b, z


def forward_kernel(
    most_ref, first_ref, vr_ref, vi_ref, row_ref, col_ref, beam_ref, high_ref, low_ref, tw_ref,
    spec_ref, sums_ref, br, bi, zr, zi, acc, grid, dh, dl, iota_ref,
):
    fill_iota(iota_ref)
    first = first_ref[0]

    def bucket_step(cp, carry):
        base = cp * CAP
        most = jnp.minimum(most_ref[cp >> 4, cp & 15], CAP)

        def tiles(t, carry):
            phase_rows(t, base, first, col_ref, br, bi, zr, zi, (vr_ref, vi_ref))
            return carry

        lax.fori_loop(0, (most + 7) >> 3, tiles, 0)
        acc[...] = jnp.zeros((128, ROWS), f32)

        def chunk(k, carry):
            left, right = [], []
            for h in range(2):
                rank = 2 * k + h
                x, z = load_phases(rank, br, bi, zr, zi)
                parts = [x]
                for _ in range(3):
                    x = cmul(x, z)
                    parts.append(x)
                value = jnp.concatenate([v[0] for v in parts] + [v[1] for v in parts], 0)
                left.append(jnp.concatenate(two_terms(value), 0))
                right.append(one_hot(row_ref, iota_ref, base + rank))
            acc[...] += lax.dot_general(
                jnp.concatenate(left, 1), jnp.concatenate(right, 1), NT, preferred_element_type=f32
            )
            return carry

        lax.fori_loop(0, (most + 1) >> 1, chunk, 0)
        grid[pl.ds(pl.multiple_of(cp * 64, 64), 64), :] = acc[0:64, :] + acc[64:128, :]
        return carry

    lax.fori_loop(0, CHANNELS * BUCKETS, bucket_step, 0)

    lane = lax.broadcasted_iota(i32, (1, LANES), 1)
    sums = jnp.zeros((1, LANES), f32)
    for c in range(CHANNELS):
        for half in range(2):
            across = slice(half * LANES, half * LANES + LANES)

            def columns(t, carry):
                x = []
                for b in range(BUCKETS):
                    at = (c * BUCKETS + b) * 64
                    x.append(
                        (
                            grid[pl.ds(pl.multiple_of(at + 8 * t, 8), 8), across],
                            grid[pl.ds(pl.multiple_of(at + 32 + 8 * t, 8), 8), across],
                        )
                    )
                y = radix16(x, -1)
                for k in range(BUCKETS):
                    turn = (
                        jnp.broadcast_to(tw_ref[0, k : k + 1, across], (8, LANES)),
                        jnp.broadcast_to(tw_ref[1, k : k + 1, across], (8, LANES)),
                    )
                    value = cmul(y[k], turn) if k else y[k]
                    at = (c * BUCKETS + k) * 64
                    grid[pl.ds(pl.multiple_of(at + 8 * t, 8), 8), across] = value[0]
                    grid[pl.ds(pl.multiple_of(at + 32 + 8 * t, 8), 8), across] = value[1]
                return carry

            lax.fori_loop(0, 4, columns, 0)
        for k in range(BUCKETS):
            at = (c * BUCKETS + k) * 64
            for part in range(2):
                high, low = two_terms(grid[at + 32 * part : at + 32 * part + 32, :])
                dh[32 * k : 32 * k + 32, ROWS * part : ROWS * part + ROWS] = high
                dl[32 * k : 32 * k + 32, ROWS * part : ROWS * part + ROWS] = low
        spec = (
            lax.dot_general(dh[...], high_ref[...], NN, preferred_element_type=f32)
            + lax.dot_general(dl[...], high_ref[...], NN, preferred_element_type=f32)
            + lax.dot_general(dh[...], low_ref[...], NN, preferred_element_type=f32)
        )
        spec_ref[c] = spec
        re, im = spec[:, 0:ROWS], spec[:, ROWS : 2 * ROWS]
        weighted = beam_ref[c] * (re * re + im * im)
        total = jnp.sum(jnp.sum(weighted, axis=0, keepdims=True), axis=1, keepdims=True)
        square = jnp.sum(jnp.sum(weighted * weighted, axis=0, keepdims=True), axis=1, keepdims=True)
        sums = jnp.where(lane == c, total, sums)
        sums = jnp.where(lane == CHANNELS + c, square, sums)

    def put(d, carry):
        sums_ref[d] = sums
        return carry

    lax.fori_loop(0, SOURCES, put, 0, unroll=8)


def adjoint_kernel(
    most_ref, first_ref, sums_ref, row_ref, col_ref, back_ref, beam_ref, high_ref, low_ref, tw_ref,
    spec_ref, out_ref, br, bi, zr, zi, tr, ti, gr, gi, grid, dh, dl, left, iota_ref,
):
    fill_iota(iota_ref)
    first = first_ref[0]
    sums = jnp.sum(sums_ref[...], axis=0)
    loss_factor = float(GRID) ** 3 * math.sqrt(SOURCES * LANES)
    for c in range(CHANNELS):
        total, square = sums[:, c : c + 1], sums[:, CHANNELS + c : CHANNELS + c + 1]
        mean = square / total
        scale = (4.0 * loss_factor) / (total * total)
        for k in range(BUCKETS):
            rows = slice(32 * k, 32 * k + 32)
            re, im = spec_ref[c, rows, 0:ROWS], spec_ref[c, rows, ROWS : 2 * ROWS]
            beam = beam_ref[c, rows, :]
            weight = beam * ((beam * (re * re + im * im) - mean) * scale)
            for part, value in enumerate((weight * re, weight * im)):
                high, low = two_terms(value)
                dh[rows, ROWS * part : ROWS * part + ROWS] = high
                dl[rows, ROWS * part : ROWS * part + ROWS] = low
        spread = (
            lax.dot_general(dh[...], high_ref[...], NT, preferred_element_type=f32)
            + lax.dot_general(dl[...], high_ref[...], NT, preferred_element_type=f32)
            + lax.dot_general(dh[...], low_ref[...], NT, preferred_element_type=f32)
        )
        for k in range(BUCKETS):
            at = (c * BUCKETS + k) * 64
            grid[at : at + 32, :] = spread[32 * k : 32 * k + 32, 0:ROWS]
            grid[at + 32 : at + 64, :] = spread[32 * k : 32 * k + 32, ROWS : 2 * ROWS]
        for half in range(2):
            across = slice(half * LANES, half * LANES + LANES)

            def columns(t, carry):
                x = []
                for k in range(BUCKETS):
                    turn = (
                        jnp.broadcast_to(tw_ref[0, k : k + 1, across], (8, LANES)),
                        -jnp.broadcast_to(tw_ref[1, k : k + 1, across], (8, LANES)),
                    )
                    at = (c * BUCKETS + k) * 64
                    value = (
                        grid[pl.ds(pl.multiple_of(at + 8 * t, 8), 8), across],
                        grid[pl.ds(pl.multiple_of(at + 32 + 8 * t, 8), 8), across],
                    )
                    x.append(cmul(value, turn) if k else value)
                y = radix16(x, 1)
                for b in range(BUCKETS):
                    at = (c * BUCKETS + b) * 64
                    grid[pl.ds(pl.multiple_of(at + 8 * t, 8), 8), across] = y[b][0]
                    grid[pl.ds(pl.multiple_of(at + 32 + 8 * t, 8), 8), across] = y[b][1]
                return carry

            lax.fori_loop(0, 4, columns, 0)

    def bucket_step(cp, carry):
        base = cp * CAP
        most = jnp.minimum(most_ref[cp >> 4, cp & 15], CAP)
        tiles_used = (most + 7) >> 3

        def tiles(t, carry):
            phase_rows(t, base, first, col_ref, br, bi, zr, zi)
            return carry

        lax.fori_loop(0, tiles_used, tiles, 0)
        high, low = two_terms(grid[pl.ds(pl.multiple_of(cp * 64, 64), 64), :])
        left[0:64, :] = high
        left[64:128, :] = low

        def chunk(k, carry):
            right = jnp.concatenate([one_hot(row_ref, iota_ref, base + 2 * k + h) for h in range(2)], 1)
            both = lax.dot_general(left[...], right, NN, preferred_element_type=f32)
            both = both[0:64, :] + both[64:128, :]
            for h in range(2):
                rank = 2 * k + h
                b, z = load_phases(rank, br, bi, zr, zi)
                g = both[:, h * LANES : h * LANES + LANES]
                a = (g[24:32, :], g[56:64, :])
                for m in (2, 1, 0):
                    a = (
                        g[8 * m : 8 * m + 8, :] + (a[0] * z[0] + a[1] * z[1]),
                        g[32 + 8 * m : 40 + 8 * m, :] + (a[1] * z[0] - a[0] * z[1]),
                    )
                to = pl.multiple_of(8 * rank, 8)
                tr[pl.ds(to, 8), :] = a[0] * b[0] + a[1] * b[1]
                ti[pl.ds(to, 8), :] = a[1] * b[0] - a[0] * b[1]
            return carry

        lax.fori_loop(0, (most + 1) >> 1, chunk, 0)

        def gather(t, carry):
            to = pl.multiple_of(base + 8 * t, 8)
            for source, target in ((tr, gr), (ti, gi)):
                value = source[pl.ds(64 * t, 8, stride=8), :]
                for s in range(1, 8):
                    value = value + source[pl.ds(64 * t + s, 8, stride=8), :]
                target[pl.ds(to, 8), :] = value
            return carry

        lax.fori_loop(0, tiles_used, gather, 0)
        return carry

    lax.fori_loop(0, CHANNELS * BUCKETS, bucket_step, 0)

    for c in range(CHANNELS):
        index = back_ref[c]
        inner, block = index & (LANES - 1), index >> 7
        for part, source in enumerate((gr, gi)):
            value = None
            for t in range(3):
                at = c * SLOTS + t * LANES
                picked = lane_pick(source[at : at + LANES, :].T, inner)
                value = picked if value is None else jnp.where(block == t, picked, value)
            out_ref[:, part * CHANNELS + c, :] = value


def finish_kernel(got_ref, place_ref, volt_ref, out_ref):
    grad = jnp.sum(got_ref[...], axis=0)
    place = place_ref[...]
    grad = lane_pick(grad, jnp.concatenate([place, place], 0))
    real = jnp.zeros((1, LANES), f32)
    imag = jnp.zeros((1, LANES), f32)
    for c in range(CHANNELS):
        g_re, g_im = grad[c : c + 1, :], grad[CHANNELS + c : CHANNELS + c + 1, :]
        v_re, v_im = volt_ref[2 * c : 2 * c + 1, :], volt_ref[2 * c + 1 : 2 * c + 2, :]
        real = real + g_re * v_re + g_im * v_im
        imag = imag + g_im * v_re - g_re * v_im
    out_ref[...] = jnp.concatenate([real, imag], 0)


def exchange(message):
    return lax.all_to_all(message, AXES, split_axis=0, concat_axis=0, tiled=True)


def shape(dims, dtype=f32):
    return jax.ShapeDtypeStruct(dims, dtype)


VMEM = pl.BlockSpec(memory_space=pltpu.VMEM)
SMEM = pl.BlockSpec(memory_space=pltpu.SMEM)
LARGE = pltpu.CompilerParams(vmem_limit_bytes=56 * 1024 * 1024)


def body(voltages, antenna_gains, receiving_tile_index, cell_index, beam_weights):
    high, low, twiddle = (jnp.asarray(t) for t in dft_tables())
    device = lax.axis_index("row") * lax.axis_size("col") + lax.axis_index("col")
    first = (device * WIDTH).astype(i32).reshape(1)
    volts = voltages.reshape(2 * CHANNELS, LANES)
    tiles = receiving_tile_index.reshape(CHANNELS, LANES)
    message, place = pl.pallas_call(
        pack_kernel,
        out_shape=(shape((SOURCES, 16, LANES)), shape((CHANNELS, LANES), i32)),
        in_specs=[VMEM] * 4,
        out_specs=(VMEM, VMEM),
    )(volts, antenna_gains, tiles, cell_index)
    got = exchange(message)
    beam = beam_weights.reshape(CHANNELS, WIDTH, ROWS, BUCKETS).transpose(0, 3, 1, 2)
    beam = beam.reshape(CHANNELS, BUCKETS * WIDTH, ROWS)
    slot = shape((CHANNELS * SLOTS, LANES))
    val_re, val_im, rows, cols, back, most = pl.pallas_call(
        slot_kernel,
        out_shape=(slot, slot, slot, slot, shape((CHANNELS, SOURCES, LANES), i32), shape((8, LANES), i32)),
        in_specs=[pl.BlockSpec(memory_space=pl.ANY)],
        out_specs=(VMEM,) * 6,
        scratch_shapes=[pltpu.VMEM((16, SOURCES, LANES), f32), pltpu.SemaphoreType.DMA((16,))],
        compiler_params=LARGE,
    )(got)
    phases = [
        pltpu.VMEM((CAP * 8, LANES), f32),
        pltpu.VMEM((CAP * 8, LANES), f32),
        pltpu.VMEM((CAP, LANES), f32),
        pltpu.VMEM((CAP, LANES), f32),
    ]
    planes = [
        pltpu.VMEM((CHANNELS * BUCKETS * 64, ROWS), f32),
        pltpu.VMEM((512, 512), bf16),
        pltpu.VMEM((512, 512), bf16),
    ]
    spectrum, sums = pl.pallas_call(
        forward_kernel,
        out_shape=(shape((CHANNELS, 512, 512)), shape((SOURCES, 1, LANES))),
        in_specs=[SMEM, SMEM] + [VMEM] * 8,
        out_specs=(VMEM, VMEM),
        scratch_shapes=phases
        + [pltpu.VMEM((128, ROWS), f32)]
        + planes
        + [pltpu.VMEM((ROWS, LANES), bf16)],
        compiler_params=LARGE,
    )(most, first, val_re, val_im, rows, cols, beam, high, low, twiddle)
    sums = exchange(sums)
    partial = pl.pallas_call(
        adjoint_kernel,
        out_shape=shape((SOURCES, 8, LANES)),
        in_specs=[SMEM, SMEM] + [VMEM] * 9,
        out_specs=VMEM,
        scratch_shapes=phases
        + [pltpu.VMEM((CAP * 8, LANES), f32)] * 2
        + [pltpu.VMEM((CHANNELS * SLOTS, LANES), f32)] * 2
        + planes
        + [pltpu.VMEM((128, ROWS), bf16), pltpu.VMEM((ROWS, LANES), bf16)],
        compiler_params=LARGE,
    )(most, first, sums, rows, cols, back, beam, high, low, twiddle, spectrum)
    home = exchange(partial)
    return pl.pallas_call(
        finish_kernel,
        out_shape=shape((2, LANES)),
        in_specs=[VMEM] * 3,
        out_specs=VMEM,
    )(home, place, volts)


def solution(mesh):
    placed = (
        P(None, None, None, AXES),
        P(None, AXES),
        P(None, AXES, None),
        P(None, AXES),
        P(None, AXES, None),
    )
    return jax.shard_map(body, mesh=mesh, in_specs=placed, out_specs=P(None, AXES), check_vma=False)
```
